128 devices in a mesh: lsec: 8 (over z, core), rsec: 16 (over y, x).
Axes of the slice: x: 4, y: 4, z: 4, core: 2. Of those that a mesh axis runs over, the one named last changes fastest.
Arguments:
- wavefunction: bfloat16 [8192, 8192], P('lsec', 'rsec'), may hold values from -6 to 6
- left_env: bfloat16 [16, 8192, 1024], P(None, 'lsec'), may hold values from -0.1875 to 0.1875
- right_env: bfloat16 [16, 8192, 512], P(None, 'rsec'), may hold values from -0.25 to 0.25
Outputs:
- hpsi: bfloat16 [8192, 8192], P('lsec', 'rsec')
The draws below stay inside these ranges and needn't reach their ends.
All inputs are finite; a program needn't handle non-finite values.
Results may differ from the reference program's by a relative error of at most 0.0053.
Values may be sent and summed in bfloat16 or wider, within the bound.
A program may use at most 128 MiB of HBM per device.

```python
import jax
import jax.numpy as jnp

BL = 1024
BR = 512
CHANNELS = 16
DL = 8192
DR = 8192
N_LSEC = 8
N_RSEC = 16


def level_of(stream_key, shape, pieces, low, top_value):
    def one(axis_at, shards_of):
        steps = jax.random.uniform(jax.random.fold_in(jax.random.fold_in(stream_key, 6), axis_at), (shards_of,), jnp.float32, low / len(pieces), top_value / len(pieces))
        return jnp.repeat(jnp.exp(steps), shape[axis_at] // shards_of).reshape((-1,) + (1,) * (len(shape) - axis_at - 1))

    gain = one(*pieces[0])
    for cut in pieces[1:]:
        gain = gain * one(*cut)
    return gain


def gaussian(rng, shape, spread, reach, split=(), kind=jnp.bfloat16):
    values = spread * jax.random.normal(rng, shape, jnp.float32)
    if split:
        values = values * level_of(rng, shape, split, -0.22, 0.18)
    return jnp.clip(values, -reach, reach).astype(kind)


def setup_inputs(seed: int = 0) -> dict:
    arg_keys = jax.random.split(jax.random.key(seed), 4)
    return {
        "wavefunction": gaussian(arg_keys[0], (DL, DR), 1.0, 6.0, ((0, 8), (1, 16))),
        "left_env": gaussian(arg_keys[1], (CHANNELS, DL, BL), BL ** -0.5, 0.1875, ((1, 8),)),
        "right_env": gaussian(arg_keys[2], (CHANNELS, DR, BR), BR ** -0.5, 0.25, ((1, 16),)),
    }


channel_shifts = (0, 1, -1, 0)


def shift_blocks(x, axis, offset):
    if offset == 0:
        return x
    count = x.shape[axis]
    if offset == 1:
        kept = jax.lax.slice_in_dim(x, 1, count, axis=axis)
        pad = jnp.zeros_like(jax.lax.slice_in_dim(x, 0, 1, axis=axis))
        return jnp.concatenate([kept, pad], axis=axis)
    kept = jax.lax.slice_in_dim(x, 0, count - 1, axis=axis)
    pad = jnp.zeros_like(jax.lax.slice_in_dim(x, 0, 1, axis=axis))
    return jnp.concatenate([pad, kept], axis=axis)


def reference(wavefunction, left_env, right_env):
    blocks = wavefunction.astype(jnp.float32).reshape(N_LSEC, BL, N_RSEC, BR)
    left_all = left_env.astype(jnp.float32).reshape(CHANNELS, N_LSEC, BL, BL)
    right_all = right_env.astype(jnp.float32).reshape(CHANNELS, N_RSEC, BR, BR)
    total = jnp.zeros((N_LSEC, BL, N_RSEC, BR), jnp.float32)
    upper_sum = jnp.zeros((N_LSEC, BL, N_RSEC, BR), jnp.float32)
    lower_sum = jnp.zeros((N_LSEC, BL, N_RSEC, BR), jnp.float32)
    for channel in range(CHANNELS):
        offset = channel_shifts[channel % 4]
        moved = shift_blocks(shift_blocks(blocks, 0, offset), 2, offset)
        partial_sum = jnp.einsum("iac,ickb->iakb", left_all[channel], moved)
        partial_sum = partial_sum.astype(jnp.bfloat16).astype(jnp.float32)
        right_moved = shift_blocks(right_all[channel], 0, offset)
        term = jnp.einsum("iakc,kcb->iakb", partial_sum, right_moved)
        if offset == 0:
            total = total + term
        elif offset == 1:
            upper_sum = upper_sum + term
        else:
            lower_sum = lower_sum + term
    upper_sum = jax.lax.optimization_barrier(upper_sum.astype(jnp.bfloat16)).astype(jnp.float32)
    lower_sum = jax.lax.optimization_barrier(lower_sum.astype(jnp.bfloat16)).astype(jnp.float32)
    total = total + upper_sum + lower_sum
    total = total.reshape(N_LSEC * BL, N_RSEC * BR)
    return total.astype(jnp.bfloat16)
```

```python
import functools

import jax
import jax.numpy as jnp
from jax import lax
from jax.experimental import pallas as pl
from jax.experimental.pallas import tpu as pltpu
from jax.sharding import PartitionSpec as P

MESH = pl.DeviceIdType.MESH
BF16 = jnp.bfloat16
F32 = jnp.float32

NEAR_ROWS = ((0, 256), (256, 256), (512, 512))
FAR_ROWS = ((0, 256), (256, 256), (512, 512))
LAST_ROWS = ((0, 512), (512, 512))


def dot(a, b):
    return jnp.dot(a, b, preferred_element_type=F32)


def kernel(
    n_i,
    n_j,
    psi_hbm,
    left_hbm,
    right_hbm,
    out_hbm,
    left,
    right,
    psi,
    part,
    total,
    term,
    arrived,
    result,
    psi_sem,
    left_sem,
    right_sem,
    psi_send,
    psi_recv,
    term_send,
    term_recv,
    out_sem,
):
    i, j = lax.axis_index("lsec"), lax.axis_index("rsec")
    odd = lax.rem(i, 2)
    near_i, far_i = i + 1 - 2 * odd, i - 1 + 2 * odd
    near_j, far_j = j - 1 + 2 * odd, j + 1 - 2 * odd
    has_far = jnp.logical_and(far_i >= 0, far_i < n_i)
    has_near_j = jnp.logical_and(near_j >= 0, near_j < n_j)
    has_far_j = jnp.logical_and(far_j >= 0, far_j < n_j)
    far_out = jnp.logical_and(has_far, has_far_j)
    far_in = jnp.logical_and(has_far, has_near_j)

    def channel(slot):
        if slot < 4:
            return 4 * slot + 1 + odd
        if slot < 8:
            return 4 * (slot - 4) + 2 - odd
        return 4 * ((slot - 8) // 2) + 3 * ((slot - 8) % 2)

    def load(slot):
        c = channel(slot)
        return (
            pltpu.make_async_copy(left_hbm.at[c], left.at[slot], left_sem.at[slot]),
            pltpu.make_async_copy(
                right_hbm.at[c], right.at[pl.ds(slot * 512, 512)], right_sem.at[slot]
            ),
        )

    def start(slots):
        for slot in slots:
            for copy in load(slot):
                copy.start()

    def await_(slots):
        for slot in slots:
            for copy in load(slot):
                copy.wait()

    own = pltpu.make_async_copy(psi_hbm, psi.at[0], psi_sem)
    own.start()
    start((8, 9))

    barrier = pltpu.get_barrier_semaphore()

    def greet(exists, device):
        @pl.when(exists)
        def _():
            pl.semaphore_signal(
                barrier, inc=1, device_id=device, device_id_type=MESH
            )

    pl.semaphore_signal(barrier, inc=1, device_id=(near_i, j), device_id_type=MESH)
    greet(has_far, (far_i, j))
    greet(has_near_j, (i, near_j))
    greet(has_far_j, (i, far_j))
    peers = 1 + sum(e.astype(jnp.int32) for e in (has_far, has_near_j, has_far_j))
    pl.semaphore_wait(barrier, peers)

    def psi_copy(k, device):
        return pltpu.make_async_remote_copy(
            src_ref=psi_hbm,
            dst_ref=psi.at[k],
            send_sem=psi_send.at[k - 1],
            recv_sem=psi_recv.at[k - 1],
            device_id=device,
            device_id_type=MESH,
        )

    near_psi = psi_copy(1, (near_i, j))
    far_psi = psi_copy(2, (far_i, j))
    near_psi.start()

    @pl.when(has_far)
    def _():
        far_psi.start()

    start((0, 1, 2, 3))

    def term_copy(k, at, rows, device):
        return pltpu.make_async_remote_copy(
            src_ref=term.at[k, pl.ds(*rows)],
            dst_ref=arrived.at[k, pl.ds(*rows)],
            send_sem=term_send.at[k, at],
            recv_sem=term_recv.at[k, at],
            device_id=device,
            device_id_type=MESH,
        )

    near_terms = [term_copy(0, a, r, (i, near_j)) for a, r in enumerate(NEAR_ROWS)]
    far_terms = [term_copy(1, a, r, (i, far_j)) for a, r in enumerate(FAR_ROWS)]

    def contract(slots, which, rows):
        first, size = rows
        for at, slot in enumerate(slots):
            part[pl.ds(0, size), at * 512 : (at + 1) * 512] = dot(
                left[slot, pl.ds(first, size), :], psi[which]
            ).astype(BF16)
        return dot(
            part[pl.ds(0, size), : len(slots) * 512],
            right[slots[0] * 512 : (slots[0] + len(slots)) * 512, :],
        )

    own.wait()
    await_((8, 9))
    total[...] = contract((8, 9), 0, (0, 1024))
    start((10, 11, 4, 5, 6, 7))

    near_psi.wait_recv()
    await_((0, 1, 2, 3))

    @pl.when(has_near_j)
    def _():
        for copy, rows in zip(near_terms, NEAR_ROWS):
            term[0, pl.ds(*rows), :] = contract((0, 1, 2, 3), 1, rows).astype(BF16)
            copy.start()

    start((12, 13, 14, 15))
    await_((10, 11))
    total[...] += contract((10, 11), 0, (0, 1024))

    await_((4, 5, 6, 7))

    @pl.when(has_far)
    def _():
        far_psi.wait_recv()

    @pl.when(far_out)
    def _():
        for copy, rows in zip(far_terms, FAR_ROWS):
            term[1, pl.ds(*rows), :] = contract((4, 5, 6, 7), 2, rows).astype(BF16)
            copy.start()

    @pl.when(jnp.logical_not(has_far_j))
    def _():
        arrived[0] = jnp.zeros((1024, 512), BF16)

    @pl.when(jnp.logical_not(far_in))
    def _():
        arrived[1] = jnp.zeros((1024, 512), BF16)

    await_((12, 13, 14, 15))
    for rows in LAST_ROWS:
        total[pl.ds(*rows), :] += contract((12, 13, 14, 15), 0, rows)

    written = []
    for at, rows in enumerate(NEAR_ROWS):

        @pl.when(has_far_j)
        def _(copy=near_terms[at]):
            copy.wait_recv()

        @pl.when(far_in)
        def _(copy=far_terms[at]):
            copy.wait_recv()

        here = pl.ds(*rows)
        result[here, :] = (
            total[here, :] + arrived[0, here, :].astype(F32) + arrived[1, here, :].astype(F32)
        ).astype(BF16)
        copy = pltpu.make_async_copy(result.at[here], out_hbm.at[here], out_sem.at[at])
        copy.start()
        written.append(copy)

    near_psi.wait_send()

    @pl.when(has_far)
    def _():
        far_psi.wait_send()

    @pl.when(has_near_j)
    def _():
        for copy in near_terms:
            copy.wait_send()

    @pl.when(far_out)
    def _():
        for copy in far_terms:
            copy.wait_send()

    for copy in written:
        copy.wait()


def solution(mesh):
    n_i, n_j = mesh.shape["lsec"], mesh.shape["rsec"]

    def shards(wavefunction, left_env, right_env):
        count, rows = left_env.shape[:2]
        columns = right_env.shape[1]
        any_space = pl.BlockSpec(memory_space=pl.ANY)
        return pl.pallas_call(
            functools.partial(kernel, n_i, n_j),
            out_shape=jax.ShapeDtypeStruct((rows, columns), BF16),
            in_specs=[any_space] * 3,
            out_specs=any_space,
            scratch_shapes=[
                pltpu.VMEM((count, rows, rows), BF16),
                pltpu.VMEM((count * columns, columns), BF16),
                pltpu.VMEM((3, rows, columns), BF16),
                pltpu.VMEM((rows, 4 * columns), BF16),
                pltpu.VMEM((rows, columns), F32),
                pltpu.VMEM((2, rows, columns), BF16),
                pltpu.VMEM((2, rows, columns), BF16),
                pltpu.VMEM((rows, columns), BF16),
                pltpu.SemaphoreType.DMA,
                pltpu.SemaphoreType.DMA((count,)),
                pltpu.SemaphoreType.DMA((count,)),
                pltpu.SemaphoreType.DMA((2,)),
                pltpu.SemaphoreType.DMA((2,)),
                pltpu.SemaphoreType.DMA((2, len(NEAR_ROWS))),
                pltpu.SemaphoreType.DMA((2, len(NEAR_ROWS))),
                pltpu.SemaphoreType.DMA((len(NEAR_ROWS),)),
            ],
            compiler_params=pltpu.CompilerParams(
                collective_id=0, has_side_effects=True, vmem_limit_bytes=62 << 20
            ),
        )(wavefunction, left_env, right_env)

    return jax.shard_map(
        shards,
        mesh=mesh,
        in_specs=(P("lsec", "rsec"), P(None, "lsec", None), P(None, "rsec", None)),
        out_specs=P("lsec", "rsec"),
        check_vma=False,
    )
```

```python
import functools

import jax
import jax.numpy as jnp
from jax import lax
from jax.experimental import pallas as pl
from jax.experimental.pallas import tpu as pltpu
from jax.sharding import PartitionSpec as P

MESH = pl.DeviceIdType.MESH
BF16 = jnp.bfloat16
F32 = jnp.float32

TERM_ROWS = ((0, 256), (256, 256), (512, 512))
NEAR_PIECES = ((0, 512), (512, 512))
FAR_PIECES = ((0, 768), (768, 256))
LAST_ROWS = ((0, 512), (512, 512))


def dot(a, b):
    return jnp.dot(a, b, preferred_element_type=F32)


def kernel(
    n_i,
    n_j,
    psi_hbm,
    left_hbm,
    right_hbm,
    out_hbm,
    left,
    right,
    psi,
    part,
    sums,
    total,
    term,
    arrived,
    psi_sem,
    left_sem,
    rows_sem,
    right_sem,
    psi_send,
    psi_recv,
    term_send,
    term_recv,
):
    i, j = lax.axis_index("lsec"), lax.axis_index("rsec")
    odd = lax.rem(i, 2)
    near_i, far_i = i + 1 - 2 * odd, i - 1 + 2 * odd
    near_j, far_j = j - 1 + 2 * odd, j + 1 - 2 * odd
    has_far = jnp.logical_and(far_i >= 0, far_i < n_i)
    has_near_j = jnp.logical_and(near_j >= 0, near_j < n_j)
    has_far_j = jnp.logical_and(far_j >= 0, far_j < n_j)
    far_out = jnp.logical_and(has_far, has_far_j)
    far_in = jnp.logical_and(has_far, has_near_j)

    def channel(slot):
        if slot < 4:
            return 4 * slot + 1 + odd
        if slot < 8:
            return 4 * (slot - 4) + 2 - odd
        return 4 * ((slot - 8) // 2) + 3 * ((slot - 8) % 2)

    def load_right(slot):
        return pltpu.make_async_copy(
            right_hbm.at[channel(slot)],
            right.at[pl.ds(slot * 512, 512)],
            right_sem.at[slot],
        )

    def load_rows(at):
        rows = pl.ds(*TERM_ROWS[at])
        return [
            pltpu.make_async_copy(
                left_hbm.at[channel(slot), rows],
                left.at[slot, rows],
                rows_sem.at[slot, at],
            )
            for slot in range(4)
        ]

    def load(slot):
        c = channel(slot)
        return (
            pltpu.make_async_copy(left_hbm.at[c], left.at[slot], left_sem.at[slot]),
            load_right(slot),
        )

    def start(slots):
        for slot in slots:
            for copy in load(slot):
                copy.start()

    def await_(slots):
        for slot in slots:
            for copy in load(slot):
                copy.wait()

    own = pltpu.make_async_copy(psi_hbm, psi.at[0], psi_sem)
    own.start()
    start((8,))
    for slot in range(4):
        load_right(slot).start()
    for at in range(1):
        for copy in load_rows(at):
            copy.start()

    barrier = pltpu.get_barrier_semaphore()

    def greet(exists, device):
        @pl.when(exists)
        def _():
            pl.semaphore_signal(
                barrier, inc=1, device_id=device, device_id_type=MESH
            )

    pl.semaphore_signal(barrier, inc=1, device_id=(near_i, j), device_id_type=MESH)
    greet(has_far, (far_i, j))
    greet(has_near_j, (i, near_j))
    greet(has_far_j, (i, far_j))
    peers = 1 + sum(e.astype(jnp.int32) for e in (has_far, has_near_j, has_far_j))
    pl.semaphore_wait(barrier, peers)

    def psi_copies(k, pieces, device):
        return [
            pltpu.make_async_remote_copy(
                src_ref=psi_hbm.at[pl.ds(*rows)],
                dst_ref=psi.at[k, pl.ds(*rows)],
                send_sem=psi_send.at[k - 1, at],
                recv_sem=psi_recv.at[k - 1, at],
                device_id=device,
                device_id_type=MESH,
            )
            for at, rows in enumerate(pieces)
        ]

    near_psi = psi_copies(1, NEAR_PIECES, (near_i, j))
    far_psi = psi_copies(2, FAR_PIECES, (far_i, j))
    for copy in near_psi:
        copy.start()

    @pl.when(has_far)
    def _():
        for copy in far_psi:
            copy.start()

    for at in range(1, len(TERM_ROWS)):
        for copy in load_rows(at):
            copy.start()

    def term_copy(k, at, rows, device):
        return pltpu.make_async_remote_copy(
            src_ref=term.at[k, pl.ds(*rows)],
            dst_ref=arrived.at[k, pl.ds(*rows)],
            send_sem=term_send.at[k, at],
            recv_sem=term_recv.at[k, at],
            device_id=device,
            device_id_type=MESH,
        )

    near_terms = [term_copy(0, a, r, (i, near_j)) for a, r in enumerate(TERM_ROWS)]
    far_terms = [term_copy(1, a, r, (i, far_j)) for a, r in enumerate(TERM_ROWS)]

    def contract(slots, which, rows):
        first, size = rows
        for at, slot in enumerate(slots):
            part[pl.ds(0, size), at * 512 : (at + 1) * 512] = dot(
                left[slot, pl.ds(first, size), :], psi[which]
            ).astype(BF16)
        return dot(
            part[pl.ds(0, size), : len(slots) * 512],
            right[slots[0] * 512 : (slots[0] + len(slots)) * 512, :],
        )

    def contract_arriving(slots, which, pieces, copies, rows):
        first, size = rows
        last = len(pieces) - 1
        for piece, (depth_first, depth) in enumerate(pieces):
            copies[piece].wait_recv()
            for at, slot in enumerate(slots):
                here = slice(at * 512, (at + 1) * 512)
                value = dot(
                    left[slot, pl.ds(first, size), depth_first : depth_first + depth],
                    psi[which, pl.ds(depth_first, depth), :],
                )
                if piece:
                    value = value + sums[pl.ds(0, size), here]
                if piece < last:
                    sums[pl.ds(0, size), here] = value
                else:
                    part[pl.ds(0, size), here] = value.astype(BF16)
        return dot(
            part[pl.ds(0, size), : len(slots) * 512],
            right[slots[0] * 512 : (slots[0] + len(slots)) * 512, :],
        )

    own.wait()
    await_((8,))
    total[...] = contract((8,), 0, (0, 1024))

    for slot in range(4):
        load_right(slot).wait()
    later = ((9, 10), (4, 5), (6, 7), ())
    for at, rows in enumerate(TERM_ROWS):
        for copy in load_rows(at):
            copy.wait()

        @pl.when(has_near_j)
        def _(at=at, rows=rows):
            slots = (0, 1, 2, 3)
            if at:
                value = contract(slots, 1, rows)
            else:
                value = contract_arriving(slots, 1, NEAR_PIECES, near_psi, rows)
            term[0, pl.ds(*rows), :] = value.astype(BF16)
            near_terms[at].start()

        start(later[at])

    @pl.when(jnp.logical_not(has_near_j))
    def _():
        for copy in near_psi:
            copy.wait_recv()

    start((11, 12, 13, 14, 15))
    await_((9, 10))
    total[...] += contract((9, 10), 0, (0, 1024))

    await_((4, 5, 6, 7))

    @pl.when(far_out)
    def _():
        slots = (4, 5, 6, 7)
        for at, rows in enumerate(TERM_ROWS):
            if at:
                value = contract(slots, 2, rows)
            else:
                value = contract_arriving(slots, 2, FAR_PIECES, far_psi, rows)
            term[1, pl.ds(*rows), :] = value.astype(BF16)
            far_terms[at].start()

    @pl.when(jnp.logical_and(has_far, jnp.logical_not(has_far_j)))
    def _():
        for copy in far_psi:
            copy.wait_recv()

    @pl.when(jnp.logical_not(has_far_j))
    def _():
        arrived[0] = jnp.zeros((1024, 512), BF16)

    @pl.when(jnp.logical_not(far_in))
    def _():
        arrived[1] = jnp.zeros((1024, 512), BF16)

    await_((11, 12, 13, 14, 15))
    for rows in LAST_ROWS:
        total[pl.ds(*rows), :] += contract((11, 12, 13, 14, 15), 0, rows)

    for at, rows in enumerate(TERM_ROWS):

        @pl.when(has_far_j)
        def _(copy=near_terms[at]):
            copy.wait_recv()

        @pl.when(far_in)
        def _(copy=far_terms[at]):
            copy.wait_recv()

        here = pl.ds(*rows)
        out_hbm[here, :] = (
            total[here, :] + arrived[0, here, :].astype(F32) + arrived[1, here, :].astype(F32)
        ).astype(BF16)

    for copy in near_psi:
        copy.wait_send()

    @pl.when(has_far)
    def _():
        for copy in far_psi:
            copy.wait_send()

    @pl.when(has_near_j)
    def _():
        for copy in near_terms:
            copy.wait_send()

    @pl.when(far_out)
    def _():
        for copy in far_terms:
            copy.wait_send()


def solution(mesh):
    n_i, n_j = mesh.shape["lsec"], mesh.shape["rsec"]

    def shards(wavefunction, left_env, right_env):
        count, rows = left_env.shape[:2]
        columns = right_env.shape[1]
        any_space = pl.BlockSpec(memory_space=pl.ANY)
        return pl.pallas_call(
            functools.partial(kernel, n_i, n_j),
            out_shape=pltpu.VMEM((rows, columns), BF16),
            in_specs=[any_space] * 3,
            out_specs=pl.BlockSpec(memory_space=pltpu.VMEM),
            scratch_shapes=[
                pltpu.VMEM((count, rows, rows), BF16),
                pltpu.VMEM((count * columns, columns), BF16),
                pltpu.VMEM((3, rows, columns), BF16),
                pltpu.VMEM((rows, 5 * columns), BF16),
                pltpu.VMEM((TERM_ROWS[0][1], 4 * columns), F32),
                pltpu.VMEM((rows, columns), F32),
                pltpu.VMEM((2, rows, columns), BF16),
                pltpu.VMEM((2, rows, columns), BF16),
                pltpu.SemaphoreType.DMA,
                pltpu.SemaphoreType.DMA((count,)),
                pltpu.SemaphoreType.DMA((4, len(TERM_ROWS))),
                pltpu.SemaphoreType.DMA((count,)),
                pltpu.SemaphoreType.DMA((2, 2)),
                pltpu.SemaphoreType.DMA((2, 2)),
                pltpu.SemaphoreType.DMA((2, len(TERM_ROWS))),
                pltpu.SemaphoreType.DMA((2, len(TERM_ROWS))),
            ],
            compiler_params=pltpu.CompilerParams(
                collective_id=0, has_side_effects=True, vmem_limit_bytes=60 << 20
            ),
        )(wavefunction, left_env, right_env)

    return jax.shard_map(
        shards,
        mesh=mesh,
        in_specs=(P("lsec", "rsec"), P(None, "lsec", None), P(None, "rsec", None)),
        out_specs=P("lsec", "rsec"),
        check_vma=False,
    )
```

```python
import functools

import jax
import jax.numpy as jnp
from jax import lax
from jax.experimental import pallas as pl
from jax.experimental.pallas import tpu as pltpu
from jax.sharding import PartitionSpec as P

MESH = pl.DeviceIdType.MESH
BF16 = jnp.bfloat16
F32 = jnp.float32

TERM_ROWS = ((0, 256), (256, 256), (512, 512))
NEAR_PIECES = ((0, 768), (768, 256))
FAR_PIECES = ((0, 768), (768, 256))
LAST_ROWS = ((0, 512), (512, 512))


def dot(a, b):
    return jnp.dot(a, b, preferred_element_type=F32)


def kernel(
    n_i,
    n_j,
    psi_hbm,
    left_hbm,
    right_hbm,
    out_hbm,
    left,
    right,
    psi,
    part,
    sums,
    total,
    term,
    arrived,
    psi_sem,
    left_sem,
    rows_sem,
    right_sem,
    psi_send,
    psi_recv,
    term_send,
    term_recv,
):
    i, j = lax.axis_index("lsec"), lax.axis_index("rsec")
    odd = lax.rem(i, 2)
    near_i, far_i = i + 1 - 2 * odd, i - 1 + 2 * odd
    near_j, far_j = j - 1 + 2 * odd, j + 1 - 2 * odd
    has_far = jnp.logical_and(far_i >= 0, far_i < n_i)
    has_near_j = jnp.logical_and(near_j >= 0, near_j < n_j)
    has_far_j = jnp.logical_and(far_j >= 0, far_j < n_j)
    far_out = jnp.logical_and(has_far, has_far_j)
    far_in = jnp.logical_and(has_far, has_near_j)

    barrier = pltpu.get_barrier_semaphore()

    def greet(exists, device):
        @pl.when(exists)
        def _():
            pl.semaphore_signal(
                barrier, inc=1, device_id=device, device_id_type=MESH
            )

    pl.semaphore_signal(barrier, inc=1, device_id=(near_i, j), device_id_type=MESH)
    greet(has_far, (far_i, j))
    greet(has_near_j, (i, near_j))
    greet(has_far_j, (i, far_j))
    def channel(slot):
        if slot < 4:
            return 4 * slot + 1 + odd
        if slot < 8:
            return 4 * (slot - 4) + 2 - odd
        return 4 * ((slot - 8) // 2) + 3 * ((slot - 8) % 2)

    def load_right(slot):
        return pltpu.make_async_copy(
            right_hbm.at[channel(slot)],
            right.at[pl.ds(slot * 512, 512)],
            right_sem.at[slot],
        )

    def load_rows(at):
        rows = pl.ds(*TERM_ROWS[at])
        return [
            pltpu.make_async_copy(
                left_hbm.at[channel(slot), rows],
                left.at[slot, rows],
                rows_sem.at[slot, at],
            )
            for slot in range(4)
        ]

    def load(slot):
        c = channel(slot)
        return (
            pltpu.make_async_copy(left_hbm.at[c], left.at[slot], left_sem.at[slot]),
            load_right(slot),
        )

    def start(slots):
        for slot in slots:
            for copy in load(slot):
                copy.start()

    def await_(slots):
        for slot in slots:
            for copy in load(slot):
                copy.wait()

    own = pltpu.make_async_copy(psi_hbm, psi.at[0], psi_sem)
    own.start()
    start((8,))
    for slot in range(4):
        load_right(slot).start()
    for at in range(1):
        for copy in load_rows(at):
            copy.start()

    peers = 1 + sum(e.astype(jnp.int32) for e in (has_far, has_near_j, has_far_j))
    pl.semaphore_wait(barrier, peers)

    def psi_copies(k, pieces, device):
        return [
            pltpu.make_async_remote_copy(
                src_ref=psi_hbm.at[pl.ds(*rows)],
                dst_ref=psi.at[k, pl.ds(*rows)],
                send_sem=psi_send.at[k - 1, at],
                recv_sem=psi_recv.at[k - 1, at],
                device_id=device,
                device_id_type=MESH,
            )
            for at, rows in enumerate(pieces)
        ]

    near_psi = psi_copies(1, NEAR_PIECES, (near_i, j))
    far_psi = psi_copies(2, FAR_PIECES, (far_i, j))
    for copy in near_psi:
        copy.start()

    @pl.when(has_far)
    def _():
        for copy in far_psi:
            copy.start()

    for at in range(1, len(TERM_ROWS)):
        for copy in load_rows(at):
            copy.start()

    def term_copy(k, at, rows, device):
        return pltpu.make_async_remote_copy(
            src_ref=term.at[k, pl.ds(*rows)],
            dst_ref=arrived.at[k, pl.ds(*rows)],
            send_sem=term_send.at[k, at],
            recv_sem=term_recv.at[k, at],
            device_id=device,
            device_id_type=MESH,
        )

    near_terms = [term_copy(0, a, r, (i, near_j)) for a, r in enumerate(TERM_ROWS)]
    far_terms = [term_copy(1, a, r, (i, far_j)) for a, r in enumerate(TERM_ROWS)]

    def contract(slots, which, rows):
        first, size = rows
        for at, slot in enumerate(slots):
            part[pl.ds(0, size), at * 512 : (at + 1) * 512] = dot(
                left[slot, pl.ds(first, size), :], psi[which]
            ).astype(BF16)
        return dot(
            part[pl.ds(0, size), : len(slots) * 512],
            right[slots[0] * 512 : (slots[0] + len(slots)) * 512, :],
        )

    def contract_arriving(slots, which, pieces, copies, rows):
        first, size = rows
        last = len(pieces) - 1
        for piece, (depth_first, depth) in enumerate(pieces):
            copies[piece].wait_recv()
            for at, slot in enumerate(slots):
                here = slice(at * 512, (at + 1) * 512)
                value = dot(
                    left[slot, pl.ds(first, size), depth_first : depth_first + depth],
                    psi[which, pl.ds(depth_first, depth), :],
                )
                if piece:
                    value = value + sums[pl.ds(0, size), here]
                if piece < last:
                    sums[pl.ds(0, size), here] = value
                else:
                    part[pl.ds(0, size), here] = value.astype(BF16)
        return dot(
            part[pl.ds(0, size), : len(slots) * 512],
            right[slots[0] * 512 : (slots[0] + len(slots)) * 512, :],
        )

    own.wait()
    await_((8,))
    total[...] = contract((8,), 0, (0, 1024))

    for slot in range(4):
        load_right(slot).wait()
    later = ((9, 10), (4, 5), (6, 7), ())
    for at, rows in enumerate(TERM_ROWS):
        for copy in load_rows(at):
            copy.wait()

        @pl.when(has_near_j)
        def _(at=at, rows=rows):
            slots = (0, 1, 2, 3)
            if at:
                value = contract(slots, 1, rows)
            else:
                value = contract_arriving(slots, 1, NEAR_PIECES, near_psi, rows)
            term[0, pl.ds(*rows), :] = value.astype(BF16)
            near_terms[at].start()

        start(later[at])

    @pl.when(jnp.logical_not(has_near_j))
    def _():
        for copy in near_psi:
            copy.wait_recv()

    start((11, 12, 13, 14, 15))
    await_((9, 10))
    total[...] += contract((9, 10), 0, (0, 1024))

    await_((4, 5, 6, 7))

    @pl.when(far_out)
    def _():
        slots = (4, 5, 6, 7)
        for at, rows in enumerate(TERM_ROWS):
            if at:
                value = contract(slots, 2, rows)
            else:
                value = contract_arriving(slots, 2, FAR_PIECES, far_psi, rows)
            term[1, pl.ds(*rows), :] = value.astype(BF16)
            far_terms[at].start()

    @pl.when(jnp.logical_and(has_far, jnp.logical_not(has_far_j)))
    def _():
        for copy in far_psi:
            copy.wait_recv()

    @pl.when(jnp.logical_not(has_far_j))
    def _():
        arrived[0] = jnp.zeros((1024, 512), BF16)

    @pl.when(jnp.logical_not(far_in))
    def _():
        arrived[1] = jnp.zeros((1024, 512), BF16)

    await_((11, 12, 13, 14, 15))
    for rows in LAST_ROWS:
        total[pl.ds(*rows), :] += contract((11, 12, 13, 14, 15), 0, rows)

    for at, rows in enumerate(TERM_ROWS):

        @pl.when(has_far_j)
        def _(copy=near_terms[at]):
            copy.wait_recv()

        @pl.when(far_in)
        def _(copy=far_terms[at]):
            copy.wait_recv()

        here = pl.ds(*rows)
        out_hbm[here, :] = (
            total[here, :] + arrived[0, here, :].astype(F32) + arrived[1, here, :].astype(F32)
        ).astype(BF16)

    for copy in near_psi:
        copy.wait_send()

    @pl.when(has_far)
    def _():
        for copy in far_psi:
            copy.wait_send()

    @pl.when(has_near_j)
    def _():
        for copy in near_terms:
            copy.wait_send()

    @pl.when(far_out)
    def _():
        for copy in far_terms:
            copy.wait_send()


def solution(mesh):
    n_i, n_j = mesh.shape["lsec"], mesh.shape["rsec"]

    def shards(wavefunction, left_env, right_env):
        count, rows = left_env.shape[:2]
        columns = right_env.shape[1]
        any_space = pl.BlockSpec(memory_space=pl.ANY)
        return pl.pallas_call(
            functools.partial(kernel, n_i, n_j),
            out_shape=pltpu.VMEM((rows, columns), BF16),
            in_specs=[any_space] * 3,
            out_specs=pl.BlockSpec(memory_space=pltpu.VMEM),
            scratch_shapes=[
                pltpu.VMEM((count, rows, rows), BF16),
                pltpu.VMEM((count * columns, columns), BF16),
                pltpu.VMEM((3, rows, columns), BF16),
                pltpu.VMEM((rows, 5 * columns), BF16),
                pltpu.VMEM((TERM_ROWS[0][1], 4 * columns), F32),
                pltpu.VMEM((rows, columns), F32),
                pltpu.VMEM((2, rows, columns), BF16),
                pltpu.VMEM((2, rows, columns), BF16),
                pltpu.SemaphoreType.DMA,
                pltpu.SemaphoreType.DMA((count,)),
                pltpu.SemaphoreType.DMA((4, len(TERM_ROWS))),
                pltpu.SemaphoreType.DMA((count,)),
                pltpu.SemaphoreType.DMA((2, 2)),
                pltpu.SemaphoreType.DMA((2, 2)),
                pltpu.SemaphoreType.DMA((2, len(TERM_ROWS))),
                pltpu.SemaphoreType.DMA((2, len(TERM_ROWS))),
            ],
            compiler_params=pltpu.CompilerParams(
                collective_id=0, has_side_effects=True, vmem_limit_bytes=60 << 20
            ),
        )(wavefunction, left_env, right_env)

    return jax.shard_map(
        shards,
        mesh=mesh,
        in_specs=(P("lsec", "rsec"), P(None, "lsec", None), P(None, "rsec", None)),
        out_specs=P("lsec", "rsec"),
        check_vma=False,
    )
```

```python
import functools

import jax
import jax.numpy as jnp
from jax import lax
from jax.experimental import pallas as pl
from jax.experimental.pallas import tpu as pltpu
from jax.sharding import PartitionSpec as P

MESH = pl.DeviceIdType.MESH
BF16 = jnp.bfloat16
F32 = jnp.float32

TERM_ROWS = ((0, 256), (256, 256), (512, 256), (768, 256))
NEAR_PIECES = ((0, 512), (512, 512))
FAR_PIECES = ((0, 768), (768, 256))
LAST_ROWS = ((0, 1024),)


def dot(a, b):
    return jnp.dot(a, b, preferred_element_type=F32)


def kernel(
    n_i,
    n_j,
    psi_hbm,
    left_hbm,
    right_hbm,
    out_hbm,
    left,
    right,
    psi,
    part,
    sums,
    total,
    term,
    arrived,
    psi_sem,
    left_sem,
    rows_sem,
    right_sem,
    psi_send,
    psi_recv,
    term_send,
    term_recv,
):
    i, j = lax.axis_index("lsec"), lax.axis_index("rsec")
    odd = lax.rem(i, 2)
    near_i, far_i = i + 1 - 2 * odd, i - 1 + 2 * odd
    near_j, far_j = j - 1 + 2 * odd, j + 1 - 2 * odd
    has_far = jnp.logical_and(far_i >= 0, far_i < n_i)
    has_near_j = jnp.logical_and(near_j >= 0, near_j < n_j)
    has_far_j = jnp.logical_and(far_j >= 0, far_j < n_j)
    far_out = jnp.logical_and(has_far, has_far_j)
    far_in = jnp.logical_and(has_far, has_near_j)

    def channel(slot):
        if slot < 4:
            return 4 * slot + 1 + odd
        if slot < 8:
            return 4 * (slot - 4) + 2 - odd
        return 4 * ((slot - 8) // 2) + 3 * ((slot - 8) % 2)

    def load_right(slot):
        return pltpu.make_async_copy(
            right_hbm.at[channel(slot)],
            right.at[pl.ds(slot * 512, 512)],
            right_sem.at[slot],
        )

    def load_rows(at):
        rows = pl.ds(*TERM_ROWS[at])
        return [
            pltpu.make_async_copy(
                left_hbm.at[channel(slot), rows],
                left.at[slot, rows],
                rows_sem.at[slot, at],
            )
            for slot in range(4)
        ]

    def load(slot):
        c = channel(slot)
        return (
            pltpu.make_async_copy(left_hbm.at[c], left.at[slot], left_sem.at[slot]),
            load_right(slot),
        )

    def start(slots):
        for slot in slots:
            for copy in load(slot):
                copy.start()

    def await_(slots):
        for slot in slots:
            for copy in load(slot):
                copy.wait()

    own = pltpu.make_async_copy(psi_hbm, psi.at[0], psi_sem)
    own.start()
    start((8,))
    for slot in range(4):
        load_right(slot).start()
    for at in range(1):
        for copy in load_rows(at):
            copy.start()

    barrier = pltpu.get_barrier_semaphore()

    def greet(exists, device):
        @pl.when(exists)
        def _():
            pl.semaphore_signal(
                barrier, inc=1, device_id=device, device_id_type=MESH
            )

    pl.semaphore_signal(barrier, inc=1, device_id=(near_i, j), device_id_type=MESH)
    greet(has_far, (far_i, j))
    greet(has_near_j, (i, near_j))
    greet(has_far_j, (i, far_j))
    peers = 1 + sum(e.astype(jnp.int32) for e in (has_far, has_near_j, has_far_j))
    pl.semaphore_wait(barrier, peers)

    def psi_copies(k, pieces, device):
        return [
            pltpu.make_async_remote_copy(
                src_ref=psi_hbm.at[pl.ds(*rows)],
                dst_ref=psi.at[k, pl.ds(*rows)],
                send_sem=psi_send.at[k - 1, at],
                recv_sem=psi_recv.at[k - 1, at],
                device_id=device,
                device_id_type=MESH,
            )
            for at, rows in enumerate(pieces)
        ]

    near_psi = psi_copies(1, NEAR_PIECES, (near_i, j))
    far_psi = psi_copies(2, FAR_PIECES, (far_i, j))
    for copy in near_psi:
        copy.start()

    @pl.when(has_far)
    def _():
        for copy in far_psi:
            copy.start()


    def term_copy(k, at, rows, device):
        return pltpu.make_async_remote_copy(
            src_ref=term.at[k, pl.ds(*rows)],
            dst_ref=arrived.at[k, pl.ds(*rows)],
            send_sem=term_send.at[k, at],
            recv_sem=term_recv.at[k, at],
            device_id=device,
            device_id_type=MESH,
        )

    near_terms = [term_copy(0, a, r, (i, near_j)) for a, r in enumerate(TERM_ROWS)]
    far_terms = [term_copy(1, a, r, (i, far_j)) for a, r in enumerate(TERM_ROWS)]

    def contract(slots, which, rows):
        first, size = rows
        for at, slot in enumerate(slots):
            part[pl.ds(0, size), at * 512 : (at + 1) * 512] = dot(
                left[slot, pl.ds(first, size), :], psi[which]
            ).astype(BF16)
        return dot(
            part[pl.ds(0, size), : len(slots) * 512],
            right[slots[0] * 512 : (slots[0] + len(slots)) * 512, :],
        )

    def contract_arriving(slots, which, pieces, copies, rows):
        first, size = rows
        last = len(pieces) - 1
        for piece, (depth_first, depth) in enumerate(pieces):
            copies[piece].wait_recv()
            for at, slot in enumerate(slots):
                here = slice(at * 512, (at + 1) * 512)
                value = dot(
                    left[slot, pl.ds(first, size), depth_first : depth_first + depth],
                    psi[which, pl.ds(depth_first, depth), :],
                )
                if piece:
                    value = value + sums[pl.ds(0, size), here]
                if piece < last:
                    sums[pl.ds(0, size), here] = value
                else:
                    part[pl.ds(0, size), here] = value.astype(BF16)
        return dot(
            part[pl.ds(0, size), : len(slots) * 512],
            right[slots[0] * 512 : (slots[0] + len(slots)) * 512, :],
        )

    own.wait()
    await_((8,))
    total[...] = contract((8,), 0, (0, 1024))
    for at in range(1, len(TERM_ROWS)):
        for copy in load_rows(at):
            copy.start()

    for slot in range(4):
        load_right(slot).wait()
    later = ((9, 10), (4, 5), (6, 7), ())
    for at, rows in enumerate(TERM_ROWS):
        for copy in load_rows(at):
            copy.wait()

        @pl.when(has_near_j)
        def _(at=at, rows=rows):
            slots = (0, 1, 2, 3)
            if at:
                value = contract(slots, 1, rows)
            else:
                value = contract_arriving(slots, 1, NEAR_PIECES, near_psi, rows)
            term[0, pl.ds(*rows), :] = value.astype(BF16)
            near_terms[at].start()

        start(later[at])

    @pl.when(jnp.logical_not(has_near_j))
    def _():
        for copy in near_psi:
            copy.wait_recv()

    start((11, 12, 13, 14, 15))
    await_((9, 10))
    total[...] += contract((9, 10), 0, (0, 1024))

    await_((4, 5, 6, 7))

    @pl.when(far_out)
    def _():
        slots = (4, 5, 6, 7)
        for at, rows in enumerate(TERM_ROWS):
            if at:
                value = contract(slots, 2, rows)
            else:
                value = contract_arriving(slots, 2, FAR_PIECES, far_psi, rows)
            term[1, pl.ds(*rows), :] = value.astype(BF16)
            far_terms[at].start()

    @pl.when(jnp.logical_and(has_far, jnp.logical_not(has_far_j)))
    def _():
        for copy in far_psi:
            copy.wait_recv()

    @pl.when(jnp.logical_not(has_far_j))
    def _():
        arrived[0] = jnp.zeros((1024, 512), BF16)

    @pl.when(jnp.logical_not(far_in))
    def _():
        arrived[1] = jnp.zeros((1024, 512), BF16)

    await_((11, 12, 13, 14, 15))
    for rows in LAST_ROWS:
        total[pl.ds(*rows), :] += contract((11, 12, 13, 14, 15), 0, rows)

    for at, rows in enumerate(TERM_ROWS):

        @pl.when(has_far_j)
        def _(copy=near_terms[at]):
            copy.wait_recv()

        @pl.when(far_in)
        def _(copy=far_terms[at]):
            copy.wait_recv()

        here = pl.ds(*rows)
        out_hbm[here, :] = (
            total[here, :] + arrived[0, here, :].astype(F32) + arrived[1, here, :].astype(F32)
        ).astype(BF16)

    for copy in near_psi:
        copy.wait_send()

    @pl.when(has_far)
    def _():
        for copy in far_psi:
            copy.wait_send()

    @pl.when(has_near_j)
    def _():
        for copy in near_terms:
            copy.wait_send()

    @pl.when(far_out)
    def _():
        for copy in far_terms:
            copy.wait_send()


def solution(mesh):
    n_i, n_j = mesh.shape["lsec"], mesh.shape["rsec"]

    def shards(wavefunction, left_env, right_env):
        count, rows = left_env.shape[:2]
        columns = right_env.shape[1]
        any_space = pl.BlockSpec(memory_space=pl.ANY)
        return pl.pallas_call(
            functools.partial(kernel, n_i, n_j),
            out_shape=pltpu.VMEM((rows, columns), BF16),
            in_specs=[any_space] * 3,
            out_specs=pl.BlockSpec(memory_space=pltpu.VMEM),
            scratch_shapes=[
                pltpu.VMEM((count, rows, rows), BF16),
                pltpu.VMEM((count * columns, columns), BF16),
                pltpu.VMEM((3, rows, columns), BF16),
                pltpu.VMEM((rows, 5 * columns), BF16),
                pltpu.VMEM((TERM_ROWS[0][1], 4 * columns), F32),
                pltpu.VMEM((rows, columns), F32),
                pltpu.VMEM((2, rows, columns), BF16),
                pltpu.VMEM((2, rows, columns), BF16),
                pltpu.SemaphoreType.DMA,
                pltpu.SemaphoreType.DMA((count,)),
                pltpu.SemaphoreType.DMA((4, len(TERM_ROWS))),
                pltpu.SemaphoreType.DMA((count,)),
                pltpu.SemaphoreType.DMA((2, 2)),
                pltpu.SemaphoreType.DMA((2, 2)),
                pltpu.SemaphoreType.DMA((2, len(TERM_ROWS))),
                pltpu.SemaphoreType.DMA((2, len(TERM_ROWS))),
            ],
            compiler_params=pltpu.CompilerParams(
                collective_id=0, has_side_effects=True, vmem_limit_bytes=60 << 20
            ),
        )(wavefunction, left_env, right_env)

    return jax.shard_map(
        shards,
        mesh=mesh,
        in_specs=(P("lsec", "rsec"), P(None, "lsec", None), P(None, "rsec", None)),
        out_specs=P("lsec", "rsec"),
        check_vma=False,
    )
```
